32 devices in a mesh: groups: 2 (over y), context: 8 (over z, x), tensor: 2 (over core).
Axes of the slice: x: 2, y: 2, z: 4, core: 2. Of those that a mesh axis runs over, the one named last changes fastest.
Arguments:
- q_raw: bfloat16 [2048, 1024], P(('groups', 'context'), 'tensor'), parts along dimension 0, may hold values from -6 to 6
- k_raw: bfloat16 [2048, 1024], P(('groups', 'context'), 'tensor'), parts along dimension 0, may hold values from -6 to 6
- v_raw: bfloat16 [2048, 2048], P(('groups', 'context'), 'tensor'), parts along dimension 0, may hold values from -6 to 6
- gate_z: bfloat16 [2048, 2048], P(('groups', 'context'), 'tensor'), parts along dimension 0, may hold values from -6 to 6
- beta_logit: float32 [2048, 16], P(('groups', 'context'), 'tensor'), parts along dimension 0
- decay_in: float32 [2048, 16], P(('groups', 'context'), 'tensor'), parts along dimension 0
- conv_q: bfloat16 [4, 1024], P(None, 'tensor'), may hold values from -3 to 3
- conv_k: bfloat16 [4, 1024], P(None, 'tensor'), may hold values from -3 to 3
- conv_v: bfloat16 [4, 2048], P(None, 'tensor'), may hold values from -3 to 3
- a_log: float32 [16], P('tensor'), may hold values from 0 to 1.1
- dt_bias: float32 [16], P('tensor'), may hold values from -0.5 to 0.5
- norm_gain: float32 [128], replicated, may hold values from 0.25 to 1.75
Outputs:
- mixed_out: bfloat16 [2048, 2048], P(('groups', 'context'), 'tensor'), parts along dimension 0
The draws below stay inside these ranges and needn't reach their ends.
There are 2 independent parts, one for each index of `groups`. The reference program is written for one: setup_inputs(seed, part) draws one part's arguments, and reference() takes and returns one part's arrays. A program takes and returns all parts, laid end to end along the dimension named above; an argument that names none is the same for every part. Nothing has to cross between parts.
All inputs are finite; a program needn't handle non-finite values.
Results may differ from the reference program's by a relative error of at most 0.0085.
Values may be sent and summed in bfloat16 or wider, within the bound.
A program may use at most 256 MiB of HBM per device.

```python
import jax
import jax.numpy as jnp
from jax import lax

TOK_DEV = 128
HK = 8
HV = 16
DK = 128
CONV = 4
SPAN = 64
TOKENS = 1024


def head_plan(key):
    marked = jax.random.fold_in(key, 11)
    head_order = jax.random.permutation(jax.random.fold_in(marked, 1), HV)
    family = head_order % 5
    low_end = 0.5
    strength_level = jax.random.uniform(jax.random.fold_in(marked, 2), (HV,), minval=low_end, maxval=1.0)
    return (family, strength_level)


def block_plan(key):
    blocks = TOKENS // TOK_DEV
    marked = jax.random.fold_in(key, 13)
    narrow_shift = jax.random.uniform(jax.random.fold_in(marked, 1), (blocks, HV), minval=-0.7, maxval=0.7)
    broad_shift = jax.random.uniform(jax.random.fold_in(marked, 2), (blocks, HV), minval=-1.0, maxval=1.0)
    quiet_score = jax.random.uniform(jax.random.fold_in(marked, 3), (blocks, HV))
    narrow_rows = jnp.repeat(narrow_shift, TOK_DEV, axis=0)
    broad_rows = jnp.repeat(broad_shift, TOK_DEV, axis=0)
    quiet_rows = jnp.repeat(quiet_score, TOK_DEV, axis=0) < 0.5
    return (narrow_rows, broad_rows, quiet_rows)


def pick_family(family, parts):
    result = parts[0]
    for index in range(1, 5):
        result = jnp.where((family == index)[None, :], parts[index], result)
    return result


def draw_beta_logit(key, part):
    family, strength_level = head_plan(key)
    narrow_rows, broad_rows, quiet_rows = block_plan(key)
    jitter = jax.random.uniform(jax.random.fold_in(key, 21), (TOKENS, HV), minval=-1.0, maxval=1.0)
    fast_part = 3.0 * jitter
    lagging_part = jnp.log(strength_level * 40.0 / TOKENS)[None, :] + 0.5 * jitter
    spread_part = jitter
    faint_part = -6.0 + 0.5 * jitter
    switch_part = jnp.where(quiet_rows, faint_part, fast_part)
    result = pick_family(family, (fast_part, lagging_part, spread_part, faint_part, switch_part))
    return result.astype(jnp.float32)


def draw_decay_in(key, part):
    family, strength_level = head_plan(key)
    narrow_rows, broad_rows, quiet_rows = block_plan(key)
    jitter = jax.random.uniform(jax.random.fold_in(key, 31), (TOKENS, HV), minval=-1.0, maxval=1.0)
    fast_part = -4.6 + narrow_rows + jitter
    lagging_part = jnp.log(strength_level * 0.15 / TOKENS)[None, :] + narrow_rows + 0.5 * jitter
    sampled_locations = jax.random.randint(jax.random.fold_in(key, 33), (2, HV), 0, TOKENS)
    sequence_indices = jnp.arange(TOKENS)[:, None]
    sudden_entries = (sequence_indices == sampled_locations[0][None, :]) | (sequence_indices == sampled_locations[1][None, :])
    lagging_part = jnp.where(sudden_entries, -1.6 + 0.3 * jitter, lagging_part)
    relay_part = jnp.log(1.5 / TOK_DEV) + broad_rows + 0.3 * jitter
    switch_part = jnp.where(quiet_rows, -12.0 + jitter, -3.5 + 0.5 * jitter)
    result = pick_family(family, (fast_part, lagging_part, lagging_part, relay_part, switch_part))
    return result.astype(jnp.float32)


def block_scale(stream_key, dims, cuts, low, top_value):
    loudness, own = 1.0, jax.random.fold_in(stream_key, 6)
    for axis_at, blocks in cuts:
        heights = jnp.exp(jax.random.uniform(jax.random.fold_in(own, axis_at), (blocks,), jnp.float32, low / len(cuts), top_value / len(cuts)))
        loudness = loudness * jnp.repeat(heights, dims[axis_at] // blocks).reshape([-1 if axis == axis_at else 1 for axis in range(len(dims))])
    return loudness


def gaussian(stream_key, shape, deviation, most, pieces=(), kind=jnp.bfloat16):
    gain = block_scale(stream_key, shape, pieces, -0.22, 0.18) if pieces else 1.0
    values = jax.random.normal(stream_key, shape, jnp.float32) * deviation * gain
    return jnp.minimum(jnp.maximum(values, -most), most).astype(kind)


def setup_inputs(seed: int = 0, part: int = 0) -> dict:
    seeds = jax.random.split(jax.random.key(seed), 13)
    part_splits = jax.random.split(jax.random.fold_in(seeds[12], part), 13)
    q_raw = gaussian(part_splits[0], (TOKENS, HK * DK), 1.0, 6.0, ((0, 8), (1, 2)))
    k_raw = gaussian(part_splits[1], (TOKENS, HK * DK), 1.0, 6.0, ((0, 8), (1, 2)))
    v_raw = gaussian(part_splits[2], (TOKENS, HV * DK), 1.0, 6.0, ((0, 8), (1, 2)))
    gate_z = gaussian(part_splits[3], (TOKENS, HV * DK), 1.0, 6.0, ((0, 8), (1, 2)))
    beta_logit = draw_beta_logit(jax.random.fold_in(jax.random.fold_in(seeds[12], part), 71), part)
    decay_in = draw_decay_in(jax.random.fold_in(jax.random.fold_in(seeds[12], part), 71), part)
    conv_q = gaussian(seeds[6], (CONV, HK * DK), CONV ** -0.5, 3.0, ((1, 2),))
    conv_k = gaussian(seeds[7], (CONV, HK * DK), CONV ** -0.5, 3.0, ((1, 2),))
    conv_v = gaussian(seeds[8], (CONV, HV * DK), CONV ** -0.5, 3.0, ((1, 2),))
    a_log = jnp.clip(1.1 * jax.random.uniform(seeds[9], (HV,), jnp.float32) ** block_scale(seeds[9], (HV,), ((0, 2),), -0.2, 0.2), 0.0, 1.1)
    dt_bias = jnp.clip(jax.random.uniform(seeds[10], (HV,), jnp.float32, -0.5, 0.5) * block_scale(seeds[10], (HV,), ((0, 2),), -0.4, 0.0), -0.5, 0.5)
    norm_gain = jnp.clip(1.0 + 0.15 * jax.random.normal(seeds[11], (DK,), jnp.float32), 0.25, 1.75)
    return {"q_raw": q_raw, "k_raw": k_raw, "v_raw": v_raw, "gate_z": gate_z, "beta_logit": beta_logit, "decay_in": decay_in, "conv_q": conv_q, "conv_k": conv_k, "conv_v": conv_v, "a_log": a_log, "dt_bias": dt_bias, "norm_gain": norm_gain}


HIGH = lax.Precision.HIGHEST

def mixing_weight(form, left, right):
    return jnp.einsum(form, left, right, precision=HIGH)

def causal_conv(rows, rim, weights):
    full = jnp.concatenate([rim, rows], axis=0).astype(jnp.float32)
    taps = weights.shape[0]
    count = rows.shape[0]
    total = jnp.zeros((count, rows.shape[1]), jnp.float32)
    for place in range(taps):
        total = total + weights[place].astype(jnp.float32)[None, :] * full[place:place + count]
    return jax.nn.silu(total).astype(jnp.bfloat16)

def prepare(query_rows, key_rows, value_rows, beta_logit, decay_in, a_log, dt_bias, size):
    rows = query_rows.shape[0]
    kheads = query_rows.shape[1] // size
    vheads = value_rows.shape[1] // size
    repeat = vheads // kheads

    def unit(block):
        block = block.astype(jnp.float32).reshape(rows, kheads, size)
        block = block / jnp.sqrt(lax.optimization_barrier(jnp.sum(block * block, axis=-1, keepdims=True)) + 1e-06)
        return jnp.repeat(block, repeat, axis=1)
    q_unit = unit(query_rows) * size ** (-0.5)
    k_unit = unit(key_rows)
    v_full = value_rows.astype(jnp.float32).reshape(rows, vheads, size)
    betas = jax.nn.sigmoid(beta_logit)
    decays = -jnp.exp(a_log)[None, :] * jax.nn.softplus(decay_in + dt_bias[None, :])
    return (q_unit, k_unit, v_full, betas, decays)

def to_blocks(array, span):
    count = array.shape[0] // span
    array = array.reshape((count, span) + array.shape[1:])
    return jnp.swapaxes(array, 1, 2)

def unpack_segments(array):
    array = jnp.swapaxes(array, 1, 2)
    return array.reshape((array.shape[0] * array.shape[1],) + array.shape[2:])

def span_parts(query_rows, key_rows, betas, decays):
    count = decays.shape[-1]
    cumul = jnp.cumsum(decays, axis=-1)
    place = jnp.arange(count)
    later = place[:, None] >= place[None, :]
    strict = place[:, None] > place[None, :]
    gap = cumul[:, :, None] - cumul[:, None, :]
    ratio = jnp.where(later[None], jnp.exp(jnp.minimum(gap, 0.0)), 0.0)
    inner = mixing_weight('hck,hdk->hcd', key_rows, key_rows)
    lower = jnp.where(strict[None], betas[:, :, None] * ratio * inner, 0.0)
    system = lower + jnp.eye(count, dtype=jnp.float32)[None]
    score_matrix = mixing_weight('hck,hdk->hcd', query_rows, key_rows) * ratio
    growth_factor = jnp.exp(cumul)
    tail_tokens = jnp.exp(cumul[:, -1:] - cumul)
    return (system, score_matrix, growth_factor, tail_tokens)

def solve_lower(system, rhs):
    count = system.shape[-1]
    unit_matrix = jnp.eye(count, dtype=system.dtype)[None]
    power = unit_matrix - system
    inverse = unit_matrix + power
    levels = (count - 1).bit_length()
    for level in range(1, levels):
        power = mixing_weight('hij,hjk->hik', power, power)
        inverse = inverse + mixing_weight('hij,hjk->hik', inverse, power)
    return mixing_weight('hij,hjk->hik', inverse, rhs)

def span_apply(state_matrix, inputs):
    query_rows, key_rows, value_rows, betas, decays = inputs
    system, score_matrix, growth_factor, tail_tokens = span_parts(query_rows, key_rows, betas, decays)
    known_prefix = value_rows - growth_factor[:, :, None] * mixing_weight('uxz,uzn->uxn', key_rows, state_matrix)
    state_update = solve_lower(system, betas[:, :, None] * known_prefix)
    output_rows = growth_factor[:, :, None] * mixing_weight('uxz,uzn->uxn', query_rows, state_matrix) + mixing_weight('jpr,jrf->jpf', score_matrix, state_update)
    last_token = growth_factor[:, -1][:, None, None]
    updated_state = last_token * state_matrix + mixing_weight('rbe,rbi->rei', key_rows, tail_tokens[:, :, None] * state_update)
    return (updated_state, output_rows)

def finish(mixed, gate_z, norm_gain):
    rows = mixed.shape[0]
    scale = jnp.sqrt(lax.optimization_barrier(jnp.mean(mixed * mixed, axis=-1, keepdims=True)) + 1e-06)
    gate = gate_z.astype(jnp.float32).reshape(mixed.shape)
    result = mixed / scale * norm_gain[None, None, :] * jax.nn.silu(gate)
    return result.reshape(rows, -1).astype(jnp.bfloat16)

def reference(q_raw, k_raw, v_raw, gate_z, beta_logit, decay_in, conv_q, conv_k, conv_v, a_log, dt_bias, norm_gain):
    size = norm_gain.shape[0]
    taps = conv_q.shape[0]
    query_rows = causal_conv(q_raw, jnp.zeros((taps - 1, q_raw.shape[1]), jnp.bfloat16), conv_q)
    key_rows = causal_conv(k_raw, jnp.zeros((taps - 1, k_raw.shape[1]), jnp.bfloat16), conv_k)
    value_rows = causal_conv(v_raw, jnp.zeros((taps - 1, v_raw.shape[1]), jnp.bfloat16), conv_v)
    prepared = prepare(query_rows, key_rows, value_rows, beta_logit, decay_in, a_log, dt_bias, size)
    inputs = tuple((to_blocks(array, SPAN) for array in prepared))
    heads = prepared[2].shape[1]
    state_matrix = jnp.zeros((heads, size, size), jnp.float32)
    final, mixer_results = lax.scan(span_apply, state_matrix, inputs)
    return finish(unpack_segments(mixer_results), gate_z, norm_gain)
```

```python
import functools

import jax
import jax.numpy as jnp
from jax import lax
from jax.experimental import pallas as pl
from jax.experimental.pallas import tpu as pltpu
from jax.sharding import PartitionSpec as P

MESH = pl.DeviceIdType.MESH
HIGH = lax.Precision.HIGHEST
RIM = 16
BF = jnp.bfloat16
F32 = jnp.float32


def mm(a, b):
    return jnp.dot(a.astype(BF), b.astype(BF), preferred_element_type=F32)


def mm_nt(a, b):
    return lax.dot_general(a.astype(BF), b.astype(BF), (((1,), (1,)), ((), ())), preferred_element_type=F32)


def mm_tn(a, b):
    return jnp.dot(a.astype(BF).T, b.astype(BF), preferred_element_type=F32)


def conv_silu(full, weights, count):
    taps = weights.shape[0]
    total = weights[0:1].astype(F32) * full(0)
    for i in range(1, taps):
        total = total + weights[i : i + 1].astype(F32) * full(i)
    return (total * jax.nn.sigmoid(total)).astype(BF)


def block_maps(qs, ks, vs, beta_logit, decay_in, a_log, dt_bias, repeat):
    rows, size = qs[0].shape
    heads = len(vs)
    kheads = len(ks)
    row = lax.broadcasted_iota(jnp.int32, (rows, rows), 0)
    col = lax.broadcasted_iota(jnp.int32, (rows, rows), 1)
    lane = lax.broadcasted_iota(jnp.int32, (rows, 128), 1)
    later = row >= col
    beta = jax.nn.sigmoid(beta_logit)
    x = decay_in + dt_bias
    soft = jnp.maximum(x, 0.0) + jnp.log1p(jnp.exp(-jnp.abs(x)))
    decay = -jnp.exp(a_log) * soft
    cum = jnp.dot(later.astype(F32), decay, precision=HIGH, preferred_element_type=F32)
    growth = jnp.exp(cum)
    tail = jnp.exp(cum[rows - 1 : rows] - cum)

    def norm(block):
        block = block.astype(F32)
        return 1.0 / jnp.sqrt(jnp.sum(block * block, axis=-1, keepdims=True) + 1e-06)

    qn = [norm(q) * size ** (-0.5) for q in qs]
    kn = [norm(k) for k in ks]
    stats = jnp.zeros((rows, 128), F32)
    for h in range(heads):
        stats = jnp.where(lane == h, cum[:, h : h + 1], stats)
        stats = jnp.where(lane == heads + h, beta[:, h : h + 1], stats)
    for j in range(kheads):
        stats = jnp.where(lane == 2 * heads + j, kn[j], stats)
    stats = stats.T
    inner = [mm_nt(k, k) for k in ks]
    cross = [mm_nt(q, k) for q, k in zip(qs, ks)]
    lower, score = [], []
    for h in range(heads):
        j = h // repeat
        cum_row, kn_row = stats[h : h + 1], stats[2 * heads + j : 2 * heads + j + 1]
        ratio = jnp.where(later, jnp.exp(jnp.minimum(cum[:, h : h + 1] - cum_row, 0.0)), 0.0) * kn_row
        lower.append(jnp.where(row > col, ratio * inner[j] * (beta[:, h : h + 1] * kn[j]), 0.0))
        score.append(ratio * cross[j] * qn[j])
    eye = (row == col).astype(F32)
    inv = [eye - jnp.where(row // 2 == col // 2, m, 0.0) for m in lower]
    step = 2
    while step < rows:
        mask = (row // (2 * step) == col // (2 * step)) & (row // step != col // step)
        edge = [mm(jnp.where(mask, lower[h], 0.0), inv[h]) for h in range(heads)]
        inv = [inv[h] - mm(inv[h], edge[h]) for h in range(heads)]
        step *= 2
    update, folded = [], []
    for h in range(heads):
        j = h // repeat
        beta_row = stats[heads + h : heads + h + 1]
        gain_row = beta_row * jnp.exp(stats[h : h + 1]) * stats[2 * heads + j : 2 * heads + j + 1]
        update.append(mm(inv[h] * beta_row, vs[h]).astype(BF))
        folded.append(mm(inv[h] * gain_row, ks[j]).astype(BF))
    result = []
    for h in range(heads):
        j = h // repeat
        key_tail = (ks[j].astype(F32) * (kn[j] * tail[:, h : h + 1])).astype(BF)
        both = jnp.concatenate([folded[h], update[h]], axis=1)
        ends = mm_tn(key_tail, both)
        inside = mm(score[h], both)
        reach = qs[j].astype(F32) * (qn[j] * growth[:, h : h + 1]) - inside[:, :size]
        last = jnp.broadcast_to(growth[rows - 1 : rows, h : h + 1], (1, 128))
        result.append((-ends[:, :size], last, ends[:, size:], reach, inside[:, size:]))
    return result


def halo_kernel(axis, n, q_ref, k_ref, v_ref, hq_ref, hk_ref, hv_ref, send_sem, recv_sem):
    me = lax.axis_index(axis)
    rows = q_ref.shape[0]
    first, last = me == 0, me == n - 1
    barrier = pltpu.get_barrier_semaphore()

    @pl.when(jnp.logical_not(first))
    def _():
        pl.semaphore_signal(barrier, inc=1, device_id={axis: me - 1}, device_id_type=MESH)

    @pl.when(jnp.logical_not(last))
    def _():
        pl.semaphore_signal(barrier, inc=1, device_id={axis: me + 1}, device_id_type=MESH)

    pl.semaphore_wait(barrier, jnp.where(first, 0, 1) + jnp.where(last, 0, 1))

    def copies(to):
        return [
            pltpu.make_async_remote_copy(
                src_ref=src.at[pl.ds(rows - RIM, RIM), :],
                dst_ref=dst,
                send_sem=send_sem.at[i],
                recv_sem=recv_sem.at[i],
                device_id={axis: to},
                device_id_type=MESH,
            )
            for i, (src, dst) in enumerate(((q_ref, hq_ref), (k_ref, hk_ref), (v_ref, hv_ref)))
        ]

    @pl.when(jnp.logical_not(last))
    def _():
        for copy in copies(me + 1):
            copy.start()

    @pl.when(first)
    def _():
        for ref in (hq_ref, hk_ref, hv_ref):
            ref[...] = jnp.zeros_like(ref)

    @pl.when(jnp.logical_not(first))
    def _():
        for copy in copies(me - 1):
            copy.wait_recv()

    @pl.when(jnp.logical_not(last))
    def _():
        for copy in copies(me + 1):
            copy.wait_send()


def local_kernel(
    q_ref, k_ref, v_ref, hq_ref, hk_ref, hv_ref, bl_ref, di_ref, wq_ref, wk_ref, wv_ref, al_ref, dt_ref,
    m_ref, g_ref, b_ref, p_ref, o_ref, fq_ref, fk_ref, fv_ref,
):
    rows = q_ref.shape[0]
    size = m_ref.shape[-1]
    taps = wq_ref.shape[0]
    blocks = []
    for x_ref, h_ref, w_ref, f_ref in (
        (q_ref, hq_ref, wq_ref, fq_ref), (k_ref, hk_ref, wk_ref, fk_ref), (v_ref, hv_ref, wv_ref, fv_ref)
    ):
        f_ref[pl.ds(0, RIM), :] = h_ref[...].astype(F32)
        f_ref[pl.ds(RIM, rows), :] = x_ref[...].astype(F32)
        parts = []
        for c in range(x_ref.shape[1] // size):
            lanes = pl.ds(c * size, size)
            parts.append(conv_silu(lambda i: f_ref[pl.ds(RIM - taps + 1 + i, rows), lanes], w_ref[:, lanes], rows))
        blocks.append(parts)
    qs, ks, vs = blocks
    maps = block_maps(qs, ks, vs, bl_ref[...], di_ref[...], al_ref[...], dt_ref[...], len(vs) // len(ks))
    for h, (move, last, base, reach, inside) in enumerate(maps):
        m_ref[h] = move.astype(BF)
        g_ref[pl.ds(h, 1), :] = last
        b_ref[h] = base
        p_ref[h] = reach.astype(BF)
        o_ref[h] = inside


def chain_kernel(
    axis, n, m_ref, g_ref, b_ref, p_ref, o_ref, z_ref, gain_ref, out_ref, held, sent, send_sem, recv_sem
):
    me = lax.axis_index(axis)
    heads, _, size = m_ref.shape
    first, last = me == 0, me == n - 1
    barrier = pltpu.get_barrier_semaphore()

    @pl.when(jnp.logical_not(first))
    def _():
        pl.semaphore_signal(barrier, inc=1, device_id={axis: me - 1}, device_id_type=MESH)

    @pl.when(jnp.logical_not(last))
    def _():
        pl.semaphore_signal(barrier, inc=1, device_id={axis: me + 1}, device_id_type=MESH)

    pl.semaphore_wait(barrier, jnp.where(first, 0, 1) + jnp.where(last, 0, 1))

    @pl.when(first)
    def _():
        held[...] = jnp.zeros_like(held)

    def hop(h, to):
        return pltpu.make_async_remote_copy(
            src_ref=sent.at[h],
            dst_ref=held.at[h],
            send_sem=send_sem.at[h],
            recv_sem=recv_sem.at[h],
            device_id={axis: to},
            device_id_type=MESH,
        )

    for h in range(heads):

        @pl.when(jnp.logical_not(first))
        def _():
            hop(h, me - 1).wait_recv()

        @pl.when(jnp.logical_not(last))
        def _():
            state = held[h]
            fresh = b_ref[h] + g_ref[pl.ds(h, 1), :] * state.astype(F32)
            fresh = fresh + jnp.dot(m_ref[h], state, preferred_element_type=F32)
            sent[h] = fresh.astype(sent.dtype)
            hop(h, me + 1).start()

    gain = gain_ref[...]
    for h in range(heads):
        lanes = pl.ds(h * size, size)
        mixed = o_ref[h] + jnp.dot(p_ref[h], held[h], preferred_element_type=F32)
        scale = lax.rsqrt(jnp.mean(mixed * mixed, axis=-1, keepdims=True) + 1e-06)
        gate = z_ref[:, lanes].astype(F32)
        out_ref[:, lanes] = (mixed * scale * gain * (gate * jax.nn.sigmoid(gate))).astype(out_ref.dtype)

    @pl.when(jnp.logical_not(last))
    def _():
        for h in range(heads):
            hop(h, me + 1).wait_send()


def vmem(count):
    return [pl.BlockSpec(memory_space=pltpu.VMEM)] * count


def per_device(n, q_raw, k_raw, v_raw, gate_z, beta_logit, decay_in, conv_q, conv_k, conv_v, a_log, dt_bias, norm_gain):
    size = norm_gain.shape[0]
    rows, width = q_raw.shape
    vwidth = v_raw.shape[1]
    heads = vwidth // size
    halos = pl.pallas_call(
        functools.partial(halo_kernel, "context", n),
        out_shape=[jax.ShapeDtypeStruct((RIM, w), BF) for w in (width, width, vwidth)],
        in_specs=[pl.BlockSpec(memory_space=pl.ANY)] * 3,
        out_specs=vmem(3),
        scratch_shapes=[pltpu.SemaphoreType.DMA((3,)), pltpu.SemaphoreType.DMA((3,))],
        compiler_params=pltpu.CompilerParams(collective_id=0, has_side_effects=True),
        name="halo",
    )(q_raw, k_raw, v_raw)
    square = (heads, size, size)
    tall = (heads, rows, size)
    maps = pl.pallas_call(
        local_kernel,
        out_shape=[
            jax.ShapeDtypeStruct(square, BF),
            jax.ShapeDtypeStruct((heads, 128), F32),
            jax.ShapeDtypeStruct(square, F32),
            jax.ShapeDtypeStruct(tall, BF),
            jax.ShapeDtypeStruct(tall, F32),
        ],
        in_specs=vmem(13),
        out_specs=vmem(5),
        scratch_shapes=[pltpu.VMEM((rows + RIM, w), F32) for w in (width, width, vwidth)],
        compiler_params=pltpu.CompilerParams(vmem_limit_bytes=48 << 20),
        name="local",
    )(q_raw, k_raw, v_raw, *halos, beta_logit, decay_in, conv_q, conv_k, conv_v, a_log[None], dt_bias[None])
    return pl.pallas_call(
        functools.partial(chain_kernel, "context", n),
        out_shape=jax.ShapeDtypeStruct((rows, vwidth), BF),
        in_specs=vmem(7),
        out_specs=pl.BlockSpec(memory_space=pltpu.VMEM),
        scratch_shapes=[
            pltpu.VMEM(square, BF),
            pltpu.VMEM(square, BF),
            pltpu.SemaphoreType.DMA((heads,)),
            pltpu.SemaphoreType.DMA((heads,)),
        ],
        compiler_params=pltpu.CompilerParams(collective_id=1, has_side_effects=True),
        name="chain",
    )(*maps, gate_z, norm_gain[None])


def solution(mesh):
    rows = P(("groups", "context"), "tensor")
    return jax.shard_map(
        functools.partial(per_device, mesh.shape["context"]),
        mesh=mesh,
        in_specs=(rows,) * 6 + (P(None, "tensor"),) * 3 + (P("tensor"),) * 2 + (P(),),
        out_specs=rows,
        check_vma=False,
    )
```

```python
import functools
import math

import jax
import jax.numpy as jnp
from jax import lax
from jax.experimental import pallas as pl
from jax.experimental.pallas import tpu as pltpu
from jax.sharding import PartitionSpec as P

MESH = pl.DeviceIdType.MESH
HIGH = lax.Precision.HIGHEST
RIM = 16
BF = jnp.bfloat16
F32 = jnp.float32


def mm(a, b):
    return jnp.dot(a.astype(BF), b.astype(BF), preferred_element_type=F32)


def mm_nt(a, b):
    return lax.dot_general(a.astype(BF), b.astype(BF), (((1,), (1,)), ((), ())), preferred_element_type=F32)


def mm_tn(a, b):
    return jnp.dot(a.astype(BF).T, b.astype(BF), preferred_element_type=F32)


def conv_silu(full, weights, count):
    taps = weights.shape[0]
    total = weights[0:1].astype(F32) * full(0)
    for i in range(1, taps):
        total = total + weights[i : i + 1].astype(F32) * full(i)
    return (total * jax.nn.sigmoid(total)).astype(BF)


def block_maps(qs, ks, vs, beta_rows, decay_rows, repeat):
    rows, size = qs[0].shape
    units = len(vs)
    row = lax.broadcasted_iota(jnp.int32, (rows, rows), 0)
    col = lax.broadcasted_iota(jnp.int32, (rows, rows), 1)
    later = row >= col
    cum_rows = jnp.dot(decay_rows, (row <= col).astype(F32), precision=HIGH, preferred_element_type=F32)
    pad = jnp.zeros((rows - 2 * units, rows), F32)
    columns = jnp.concatenate([cum_rows, beta_rows, pad], axis=0).T
    cum, beta = columns[:, :units], columns[:, units : 2 * units]
    growth = jnp.exp(cum)
    tail = jnp.exp(cum[rows - 1 : rows] - cum)

    def norm(block):
        block = block.astype(F32)
        return 1.0 / jnp.sqrt(jnp.sum(block * block, axis=-1, keepdims=True) + 1e-06)

    qn = [norm(q) * size ** (-0.5) for q in qs]
    kn = [norm(k) for k in ks]
    kn_rows = jnp.zeros((rows, rows), F32)
    for j, column in enumerate(kn):
        kn_rows = jnp.where(col == j, column, kn_rows)
    kn_rows = kn_rows.T
    inner = [mm_nt(k, k) for k in ks]
    cross = [mm_nt(q, k) for q, k in zip(qs, ks)]
    lower, score = [], []
    for h in range(units):
        j = h // repeat
        ratio = jnp.exp(jnp.minimum(cum[:, h : h + 1] - cum_rows[h : h + 1], 0.0))
        ratio = jnp.where(later, ratio, 0.0) * kn_rows[j : j + 1]
        lower.append(jnp.where(row > col, ratio * inner[j] * (beta[:, h : h + 1] * kn[j]), 0.0))
        score.append((ratio * cross[j] * qn[j]).astype(BF))
    eye = (row == col).astype(F32)
    inv = [eye - jnp.where(row // 2 == col // 2, m, 0.0) for m in lower]
    step = 2
    while step < rows:
        mask = (row // (2 * step) == col // (2 * step)) & (row // step != col // step)
        edge = [mm(jnp.where(mask, lower[h], 0.0), inv[h]) for h in range(units)]
        inv = [inv[h] - mm(inv[h], edge[h]) for h in range(units)]
        step *= 2
    update, folded = [], []
    for h in range(units):
        j = h // repeat
        beta_row = beta_rows[h : h + 1]
        gain_row = beta_row * jnp.exp(cum_rows[h : h + 1]) * kn_rows[j : j + 1]
        update.append(mm(inv[h] * beta_row, vs[h]).astype(BF))
        folded.append(mm(inv[h] * gain_row, ks[j]).astype(BF))
    result = []
    for h in range(units):
        j = h // repeat
        key_tail = (ks[j].astype(F32) * (kn[j] * tail[:, h : h + 1])).astype(BF)
        both = jnp.concatenate([folded[h], update[h]], axis=1)
        ends = mm_tn(key_tail, both)
        inside = mm(score[h], both)
        reach = qs[j].astype(F32) * (qn[j] * growth[:, h : h + 1]) - inside[:, :size]
        last = jnp.broadcast_to(growth[rows - 1 : rows, h : h + 1], (1, size))
        result.append((-ends[:, :size], last, ends[:, size:], reach, inside[:, size:]))
    return result


def mixer_kernel(
    axis, n, team, size,
    q_ref, k_ref, v_ref, bl_ref, di_ref, wq_ref, wk_ref, wv_ref, al_ref, dt_ref, gain_ref,
    out_ref,
    q_rows, k_rows, v_rows, logits, inputs, wq, wk, wv, al, dt, gain,
    fq, fk, fv, m_s, g_s, b_s, p_s, o_s, held, sent, back,
    local_sem, send_sem, recv_sem, rim_send, rim_recv, hop_send, hop_recv, back_send, back_recv,
):
    me = lax.axis_index(axis)
    place, turn = lax.rem(me, team), me // team
    base = turn * team
    rows = q_ref.shape[0]
    taps = wq_ref.shape[0]
    kw, vw = wq_ref.shape[1] // team, wv_ref.shape[1] // team
    kpm, hpm = kw // size, vw // size
    repeat = hpm // kpm
    units = team * hpm
    first, last = turn == 0, turn == n // team - 1
    tail_place = place == team - 1
    streams = ((q_ref, q_rows, kw), (k_ref, k_rows, kw), (v_ref, v_rows, vw))
    whole = ((bl_ref, logits), (di_ref, inputs))

    def lanes_of(who, width):
        return pl.ds(pl.multiple_of(who * width, width), width)

    def rows_of(who):
        return pl.ds(pl.multiple_of(RIM + who * rows, RIM), rows)

    staying = []
    for i, (src, dst, width) in enumerate(streams):
        staying.append((src.at[:, lanes_of(place, width)], dst.at[rows_of(place), :]))
    for src, dst in whole:
        staying.append((src, dst.at[place]))
    for src, dst, width in ((wq_ref, wq, kw), (wk_ref, wk, kw), (wv_ref, wv, vw)):
        staying.append((src.at[:, lanes_of(place, width)], dst))
    staying += [(al_ref, al), (dt_ref, dt), (gain_ref, gain)]
    staying = [pltpu.make_async_copy(a, b, local_sem.at[i]) for i, (a, b) in enumerate(staying)]
    for copy in staying:
        copy.start()

    barrier = pltpu.get_barrier_semaphore()

    def greet(who):
        pl.semaphore_signal(barrier, inc=1, device_id={axis: who}, device_id_type=MESH)

    for d in range(1, team):
        greet(base + lax.rem(place + d, team))

    @pl.when(jnp.logical_not(last))
    def _():
        greet(me + team)

        @pl.when(tail_place)
        def _():
            for p in range(team - 1):
                greet(base + team + p)

    @pl.when(jnp.logical_not(first))
    def _():
        greet(me - team)

        @pl.when(jnp.logical_not(tail_place))
        def _():
            greet(base - 1)

    ahead = jnp.where(tail_place, team, 1)
    behind = jnp.where(tail_place, 1, 2)
    pl.semaphore_wait(barrier, team - 1 + jnp.where(last, 0, ahead) + jnp.where(first, 0, behind))

    def remote(src, dst, send, recv, to):
        return pltpu.make_async_remote_copy(
            src_ref=src, dst_ref=dst, send_sem=send, recv_sem=recv, device_id={axis: to}, device_id_type=MESH
        )

    def exchange(d):
        to = lax.rem(place + d, team)
        pairs = [(src.at[:, lanes_of(to, width)], dst.at[rows_of(place), :]) for src, dst, width in streams]
        pairs += [(src, dst.at[place]) for src, dst in whole]
        return [
            remote(a, b, send_sem.at[d - 1, i], recv_sem.at[d - 1, i], base + to) for i, (a, b) in enumerate(pairs)
        ]

    def arrival(d):
        who = lax.rem(place + team - d, team)
        pairs = [(src.at[:, lanes_of(place, width)], dst.at[rows_of(who), :]) for src, dst, width in streams]
        pairs += [(src, dst.at[who]) for src, dst in whole]
        return [
            remote(a, b, send_sem.at[d - 1, i], recv_sem.at[d - 1, i], base + who) for i, (a, b) in enumerate(pairs)
        ]

    def rim(p, to):
        return [
            remote(
                src.at[pl.ds(rows - RIM, RIM), pl.ds(p * width, width)], dst.at[pl.ds(0, RIM), :],
                rim_send.at[p, i], rim_recv.at[i], to,
            )
            for i, (src, dst, width) in enumerate(streams)
        ]

    for d in range(1, team):
        for copy in exchange(d):
            copy.start()

    @pl.when(tail_place & jnp.logical_not(last))
    def _():
        for p in range(team):
            for copy in rim(p, base + team + p):
                copy.start()

    @pl.when(first)
    def _():
        for _, dst, _ in streams:
            dst[pl.ds(0, RIM), :] = jnp.zeros((RIM, dst.shape[1]), BF)
        held[...] = jnp.zeros_like(held)

    for copy in staying:
        copy.wait()

    @pl.when(jnp.logical_not(first))
    def _():
        for copy in rim(0, base - 1):
            copy.wait_recv()

    for d in range(1, team):
        for copy in arrival(d):
            copy.wait_recv()

    blocks = []
    for src, w_ref, f_ref, count in ((q_rows, wq, fq, kpm), (k_rows, wk, fk, kpm), (v_rows, wv, fv, hpm)):
        f_ref[...] = src[...].astype(F32)
        parts = []
        for b in range(team):
            for c in range(count):
                lanes = pl.ds(c * size, size)
                parts.append(
                    conv_silu(
                        lambda i: f_ref[pl.ds(RIM - taps + 1 + i + b * rows, rows), lanes], w_ref[:, lanes], rows
                    )
                )
        blocks.append(parts)
    qs, ks, vs = blocks

    heads = bl_ref.shape[0]
    diag = lax.broadcasted_iota(jnp.int32, (heads, heads), 0) == lax.broadcasted_iota(jnp.int32, (heads, heads), 1)

    def upright(ref):
        return jnp.sum(jnp.where(diag, ref[...], 0.0), axis=1, keepdims=True)

    scale_up, shift = jnp.exp(upright(al)), upright(dt)
    beta_rows, decay_rows = [], []
    for b in range(team):
        x = inputs[b] + shift
        decay = -scale_up * (jnp.maximum(x, 0.0) + jnp.log1p(jnp.exp(-jnp.abs(x))))
        beta = jax.nn.sigmoid(logits[b])
        for h in range(hpm):
            pick_b, pick_d = beta[h : h + 1], decay[h : h + 1]
            for p in range(1, team):
                at = p * hpm + h
                pick_b = jnp.where(place == p, beta[at : at + 1], pick_b)
                pick_d = jnp.where(place == p, decay[at : at + 1], pick_d)
            beta_rows.append(pick_b)
            decay_rows.append(pick_d)
    beta_rows = jnp.concatenate(beta_rows, axis=0)
    decay_rows = jnp.concatenate(decay_rows, axis=0)
    for u, (move, end, grow, reach, inside) in enumerate(block_maps(qs, ks, vs, beta_rows, decay_rows, repeat)):
        m_s[u] = move.astype(BF)
        g_s[pl.ds(u, 1), :] = end
        b_s[u] = grow
        p_s[u] = reach.astype(BF)
        o_s[u] = inside

    def hop(h, to):
        return remote(sent.at[h], held.at[h], hop_send.at[h], hop_recv.at[h], to)

    @pl.when(jnp.logical_not(first))
    def _():
        for h in range(hpm):
            hop(h, me - team).wait_recv()

    states = [held[h].astype(F32) for h in range(hpm)]
    starts = []
    for b in range(team):
        for h in range(hpm):
            u = b * hpm + h
            low = states[h].astype(BF)
            starts.append(low)
            states[h] = (
                b_s[u] + g_s[pl.ds(u, 1), :] * states[h] + jnp.dot(m_s[u], low, preferred_element_type=F32)
            )

    @pl.when(jnp.logical_not(last))
    def _():
        for h in range(hpm):
            sent[h] = states[h].astype(BF)
            hop(h, me + team).start()

    def home(b, to):
        return remote(back.at[b], out_ref.at[:, lanes_of(place, vw)], back_send.at[b], back_recv.at[place], to)

    for b in range(team):
        for h in range(hpm):
            u = b * hpm + h
            mixed = o_s[u] + jnp.dot(p_s[u], starts[u], preferred_element_type=F32)
            scale = lax.rsqrt(jnp.mean(mixed * mixed, axis=-1, keepdims=True) + 1e-06)
            back[b, :, pl.ds(h * size, size)] = (mixed * scale * gain[...]).astype(BF)

        @pl.when(place != b)
        def _():
            home(b, base + b).start()

        @pl.when(place == b)
        def _():
            out_ref[:, lanes_of(place, vw)] = back[b]

    for p in range(team):

        @pl.when(place != p)
        def _():
            remote(
                back.at[p], out_ref.at[:, pl.ds(p * vw, vw)], back_send.at[p], back_recv.at[p], base + p
            ).wait_recv()
            home(p, base + p).wait_send()

    for d in range(1, team):
        for copy in exchange(d):
            copy.wait_send()

    @pl.when(tail_place & jnp.logical_not(last))
    def _():
        for p in range(team):
            for copy in rim(p, base + team + p):
                copy.wait_send()

    @pl.when(jnp.logical_not(last))
    def _():
        for h in range(hpm):
            hop(h, me + team).wait_send()


def per_device(n, q_raw, k_raw, v_raw, gate_z, beta_logit, decay_in, conv_q, conv_k, conv_v, a_log, dt_bias, norm_gain):
    size = norm_gain.shape[0]
    rows, width = q_raw.shape
    vwidth = v_raw.shape[1]
    heads = vwidth // size
    taps = conv_q.shape[0]
    team = math.gcd(n, width // size)
    kw, vw = width // team, vwidth // team
    hpm = vw // size
    units = team * hpm
    long = RIM + team * rows
    dma = pltpu.SemaphoreType.DMA
    normed = pl.pallas_call(
        functools.partial(mixer_kernel, "context", n, team, size),
        out_shape=jax.ShapeDtypeStruct((rows, vwidth), BF),
        in_specs=[pl.BlockSpec(memory_space=pltpu.HBM)] * 11,
        out_specs=pl.BlockSpec(memory_space=pltpu.VMEM),
        scratch_shapes=[
            pltpu.VMEM((long, kw), BF),
            pltpu.VMEM((long, kw), BF),
            pltpu.VMEM((long, vw), BF),
            pltpu.VMEM((team, heads, rows), F32),
            pltpu.VMEM((team, heads, rows), F32),
            pltpu.VMEM((taps, kw), BF),
            pltpu.VMEM((taps, kw), BF),
            pltpu.VMEM((taps, vw), BF),
            pltpu.VMEM((1, heads), F32),
            pltpu.VMEM((1, heads), F32),
            pltpu.VMEM((1, size), F32),
            pltpu.VMEM((long, kw), F32),
            pltpu.VMEM((long, kw), F32),
            pltpu.VMEM((long, vw), F32),
            pltpu.VMEM((units, size, size), BF),
            pltpu.VMEM((units, size), F32),
            pltpu.VMEM((units, size, size), F32),
            pltpu.VMEM((units, rows, size), BF),
            pltpu.VMEM((units, rows, size), F32),
            pltpu.VMEM((hpm, size, size), BF),
            pltpu.VMEM((hpm, size, size), BF),
            pltpu.VMEM((team, rows, vw), BF),
            dma((11,)),
            dma((team, 5)),
            dma((team, 5)),
            dma((team, 3)),
            dma((3,)),
            dma((hpm,)),
            dma((hpm,)),
            dma((team,)),
            dma((team,)),
        ],
        compiler_params=pltpu.CompilerParams(
            collective_id=0, has_side_effects=True, vmem_limit_bytes=48 << 20
        ),
        name="mixer",
    )(
        q_raw, k_raw, v_raw, beta_logit.T, decay_in.T, conv_q, conv_k, conv_v,
        a_log[None], dt_bias[None], norm_gain[None],
    )
    return (normed.astype(F32) * jax.nn.silu(gate_z.astype(F32))).astype(BF)


def solution(mesh):
    rows = P(("groups", "context"), "tensor")
    return jax.shard_map(
        functools.partial(per_device, mesh.shape["context"]),
        mesh=mesh,
        in_specs=(rows,) * 6 + (P(None, "tensor"),) * 3 + (P("tensor"),) * 2 + (P(),),
        out_specs=rows,
        check_vma=False,
    )
```

```python
import functools
import math

import jax
import jax.numpy as jnp
from jax import lax
from jax.experimental import pallas as pl
from jax.experimental.pallas import tpu as pltpu
from jax.sharding import PartitionSpec as P

MESH = pl.DeviceIdType.MESH
HIGH = lax.Precision.HIGHEST
RIM = 16
BF = jnp.bfloat16
F32 = jnp.float32


def mm(a, b):
    return jnp.dot(a.astype(BF), b.astype(BF), preferred_element_type=F32)


def mm_nt(a, b):
    return lax.dot_general(a.astype(BF), b.astype(BF), (((1,), (1,)), ((), ())), preferred_element_type=F32)


def mm_tn(a, b):
    return jnp.dot(a.astype(BF).T, b.astype(BF), preferred_element_type=F32)


def conv_silu(full, weights, count):
    taps = weights.shape[0]
    total = weights[0:1].astype(F32) * full(0)
    for i in range(1, taps):
        total = total + weights[i : i + 1].astype(F32) * full(i)
    return (total * jax.nn.sigmoid(total)).astype(BF)


def norm(block):
    block = block.astype(F32)
    return 1.0 / jnp.sqrt(jnp.sum(block * block, axis=-1, keepdims=True) + 1e-06)


def masks(rows):
    row = lax.broadcasted_iota(jnp.int32, (rows, rows), 0)
    col = lax.broadcasted_iota(jnp.int32, (rows, rows), 1)
    return row, col


def key_stage(ks, beta_rows, decay_rows, repeat):
    rows = ks[0].shape[0]
    units = beta_rows.shape[0]
    row, col = masks(rows)
    later = row >= col
    cum_rows = jnp.dot(decay_rows, (row <= col).astype(F32), precision=HIGH, preferred_element_type=F32)
    pad = jnp.zeros((rows - 2 * units, rows), F32)
    columns = jnp.concatenate([cum_rows, beta_rows, pad], axis=0).T
    cum, beta = columns[:, :units], columns[:, units : 2 * units]
    kn = [norm(k) for k in ks]
    kn_rows = jnp.zeros((rows, rows), F32)
    for j, column in enumerate(kn):
        kn_rows = jnp.where(col == j, column, kn_rows)
    kn_rows = kn_rows.T
    inner = [mm_nt(k, k) for k in ks]
    lower, ratios = [], []
    for h in range(units):
        j = h // repeat
        ratio = jnp.exp(jnp.minimum(cum[:, h : h + 1] - cum_rows[h : h + 1], 0.0))
        ratio = jnp.where(later, ratio, 0.0) * kn_rows[j : j + 1]
        lower.append(jnp.where(row > col, ratio * inner[j] * (beta[:, h : h + 1] * kn[j]), 0.0))
        ratios.append(ratio)
    eye = (row == col).astype(F32)
    inv = [eye - jnp.where(row // 2 == col // 2, m, 0.0) for m in lower]
    step = 2
    while step < rows:
        mask = (row // (2 * step) == col // (2 * step)) & (row // step != col // step)
        edge = [mm(jnp.where(mask, lower[h], 0.0), inv[h]) for h in range(units)]
        inv = [inv[h] - mm(inv[h], edge[h]) for h in range(units)]
        step *= 2
    return cum, cum_rows, kn, kn_rows, ratios, inv


def mixer_kernel(
    axis, n, team, size,
    q_ref, k_ref, v_ref, bl_ref, di_ref, wq_ref, wk_ref, wv_ref, al_ref, dt_ref, gain_ref,
    out_ref,
    q_rows, k_rows, v_rows, logits, inputs, wq, wk, wv, al, dt, gain,
    fq, fk, fv, m_s, g_s, b_s, r_s, w_s, s_s, held, sent, back,
    local_sem, send_sem, recv_sem, rim_send, rim_recv, hop_send, hop_recv, back_send, back_recv,
):
    me = lax.axis_index(axis)
    place, turn = lax.rem(me, team), me // team
    base = turn * team
    rows = q_ref.shape[0]
    taps = wq_ref.shape[0]
    kw, vw = wq_ref.shape[1] // team, wv_ref.shape[1] // team
    kpm, hpm = kw // size, vw // size
    repeat = hpm // kpm
    units = team * hpm
    first, last = turn == 0, turn == n // team - 1
    tail_place = place == team - 1
    streams = ((k_ref, k_rows, kw), (v_ref, v_rows, vw), (q_ref, q_rows, kw))
    plans = ((k_rows, wk, fk, kpm), (v_rows, wv, fv, hpm), (q_rows, wq, fq, kpm))
    whole = ((bl_ref, logits), (di_ref, inputs))

    def lanes_of(who, width):
        return pl.ds(pl.multiple_of(who * width, width), width)

    def rows_of(who):
        return pl.ds(pl.multiple_of(RIM + who * rows, RIM), rows)

    staying = []
    for i, (src, dst, width) in enumerate(streams):
        staying.append((src.at[:, lanes_of(place, width)], dst.at[rows_of(place), :]))
    for src, dst in whole:
        staying.append((src, dst.at[place]))
    for src, dst, width in ((wq_ref, wq, kw), (wk_ref, wk, kw), (wv_ref, wv, vw)):
        staying.append((src.at[:, lanes_of(place, width)], dst))
    staying += [(al_ref, al), (dt_ref, dt), (gain_ref, gain)]
    staying = [pltpu.make_async_copy(a, b, local_sem.at[i]) for i, (a, b) in enumerate(staying)]
    for copy in staying:
        copy.start()

    barrier = pltpu.get_barrier_semaphore()

    def greet(who):
        pl.semaphore_signal(barrier, inc=1, device_id={axis: who}, device_id_type=MESH)

    for d in range(1, team):
        greet(base + lax.rem(place + d, team))

    @pl.when(jnp.logical_not(last))
    def _():
        greet(me + team)

        @pl.when(tail_place)
        def _():
            for p in range(team - 1):
                greet(base + team + p)

    @pl.when(jnp.logical_not(first))
    def _():
        greet(me - team)

        @pl.when(jnp.logical_not(tail_place))
        def _():
            greet(base - 1)

    ahead = jnp.where(tail_place, team, 1)
    behind = jnp.where(tail_place, 1, 2)
    pl.semaphore_wait(barrier, team - 1 + jnp.where(last, 0, ahead) + jnp.where(first, 0, behind))

    def remote(src, dst, send, recv, to):
        return pltpu.make_async_remote_copy(
            src_ref=src, dst_ref=dst, send_sem=send, recv_sem=recv, device_id={axis: to}, device_id_type=MESH
        )

    def exchange(d):
        to = lax.rem(place + d, team)
        pairs = [(src.at[:, lanes_of(to, width)], dst.at[rows_of(place), :]) for src, dst, width in streams]
        pairs += [(src, dst.at[place]) for src, dst in whole]
        return [
            remote(a, b, send_sem.at[d - 1, i], recv_sem.at[d - 1, i], base + to) for i, (a, b) in enumerate(pairs)
        ]

    def arrival(d):
        who = lax.rem(place + team - d, team)
        pairs = [(src.at[:, lanes_of(place, width)], dst.at[rows_of(who), :]) for src, dst, width in streams]
        pairs += [(src, dst.at[who]) for src, dst in whole]
        return [
            remote(a, b, send_sem.at[d - 1, i], recv_sem.at[d - 1, i], base + who) for i, (a, b) in enumerate(pairs)
        ]

    def rim(p, to, i):
        src, dst, width = streams[i]
        return remote(
            src.at[pl.ds(rows - RIM, RIM), pl.ds(p * width, width)], dst.at[pl.ds(0, RIM), :],
            rim_send.at[p, i], rim_recv.at[i], to,
        )

    sends = [exchange(d) for d in range(1, team)]
    takes = [arrival(d) for d in range(1, team)]
    order = (3, 4, 0, 1, 2)
    for i in order:
        for copies in sends:
            copies[i].start()
        if i < len(streams):

            @pl.when(tail_place & jnp.logical_not(last))
            def _():
                for p in range(team):
                    rim(p, base + team + p, i).start()

    @pl.when(first)
    def _():
        for _, dst, _ in streams:
            dst[pl.ds(0, RIM), :] = jnp.zeros((RIM, dst.shape[1]), BF)
        held[...] = jnp.zeros_like(held)

    for copy in staying[len(streams) :]:
        copy.wait()
    for i in (3, 4):
        for copies in takes:
            copies[i].wait_recv()

    def stream(i):
        staying[i].wait()

        @pl.when(jnp.logical_not(first))
        def _():
            rim(0, base - 1, i).wait_recv()

        for copies in takes:
            copies[i].wait_recv()
        src, w_ref, f_ref, count = plans[i]
        f_ref[...] = src[...].astype(F32)
        parts = []
        for b in range(team):
            for c in range(count):
                lanes = pl.ds(c * size, size)
                parts.append(
                    conv_silu(
                        lambda i: f_ref[pl.ds(RIM - taps + 1 + i + b * rows, rows), lanes], w_ref[:, lanes], rows
                    )
                )
        return parts

    heads = bl_ref.shape[0]
    diag = lax.broadcasted_iota(jnp.int32, (heads, heads), 0) == lax.broadcasted_iota(jnp.int32, (heads, heads), 1)

    def upright(ref):
        return jnp.sum(jnp.where(diag, ref[...], 0.0), axis=1, keepdims=True)

    scale_up, shift = jnp.exp(upright(al)), upright(dt)
    beta_rows, decay_rows = [], []
    for b in range(team):
        x = inputs[b] + shift
        decay = -scale_up * (jnp.maximum(x, 0.0) + jnp.log1p(jnp.exp(-jnp.abs(x))))
        beta = jax.nn.sigmoid(logits[b])
        for h in range(hpm):
            pick_b, pick_d = beta[h : h + 1], decay[h : h + 1]
            for p in range(1, team):
                at = p * hpm + h
                pick_b = jnp.where(place == p, beta[at : at + 1], pick_b)
                pick_d = jnp.where(place == p, decay[at : at + 1], pick_d)
            beta_rows.append(pick_b)
            decay_rows.append(pick_d)
    beta_rows = jnp.concatenate(beta_rows, axis=0)
    decay_rows = jnp.concatenate(decay_rows, axis=0)
    ks = stream(0)
    cum, cum_rows, kn, kn_rows, ratios, inv = key_stage(ks, beta_rows, decay_rows, repeat)
    growth = jnp.exp(cum)
    tail = jnp.exp(cum[rows - 1 : rows] - cum)
    for u in range(units):
        r_s[u] = ratios[u]
        beta_row = beta_rows[u : u + 1]
        gain_row = beta_row * jnp.exp(cum_rows[u : u + 1]) * kn_rows[u // repeat : u // repeat + 1]
        w_s[u, :, pl.ds(0, size)] = mm(inv[u] * gain_row, ks[u // repeat]).astype(BF)
    inv = [(inv[u] * beta_rows[u : u + 1]).astype(BF) for u in range(units)]
    vs = stream(1)
    for u in range(units):
        w_s[u, :, pl.ds(size, size)] = mm(inv[u], vs[u]).astype(BF)
    for u in range(units):
        key_tail = (ks[u // repeat].astype(F32) * (kn[u // repeat] * tail[:, u : u + 1])).astype(BF)
        ends = mm_tn(key_tail, w_s[u])
        m_s[u] = (-ends[:, :size]).astype(BF)
        b_s[u] = ends[:, size:]
        g_s[pl.ds(u, 1), :] = jnp.broadcast_to(growth[rows - 1 : rows, u : u + 1], (1, size))

    def hop(h, to):
        return remote(sent.at[h], held.at[h], hop_send.at[h], hop_recv.at[h], to)

    def carry():
        states = [held[h].astype(F32) for h in range(hpm)]
        for b in range(team):
            for h in range(hpm):
                u = b * hpm + h
                low = states[h].astype(BF)
                s_s[u] = low
                states[h] = (
                    b_s[u] + g_s[pl.ds(u, 1), :] * states[h] + jnp.dot(m_s[u], low, preferred_element_type=F32)
                )

        @pl.when(jnp.logical_not(last))
        def _():
            for h in range(hpm):
                sent[h] = states[h].astype(BF)
                hop(h, me + team).start()

    @pl.when(first)
    def _():
        carry()

    qs = stream(2)
    cross = [mm_nt(q, k) for q, k in zip(qs, ks)]
    qn = [norm(q) * size ** (-0.5) for q in qs]
    reach, within = [], []
    for u in range(units):
        j = u // repeat
        inside = mm(r_s[u] * cross[j] * qn[j], w_s[u])
        reach.append((qs[j].astype(F32) * (qn[j] * growth[:, u : u + 1]) - inside[:, :size]).astype(BF))
        within.append(inside[:, size:])

    @pl.when(jnp.logical_not(first))
    def _():
        for h in range(hpm):
            hop(h, me - team).wait_recv()
        carry()

    def home(b, to):
        return remote(back.at[b], out_ref.at[:, lanes_of(place, vw)], back_send.at[b], back_recv.at[place], to)

    for b in range(team):
        for h in range(hpm):
            u = b * hpm + h
            mixed = within[u] + jnp.dot(reach[u], s_s[u], preferred_element_type=F32)
            scale = lax.rsqrt(jnp.mean(mixed * mixed, axis=-1, keepdims=True) + 1e-06)
            back[b, :, pl.ds(h * size, size)] = (mixed * scale * gain[...]).astype(BF)

        @pl.when(place != b)
        def _():
            home(b, base + b).start()

        @pl.when(place == b)
        def _():
            out_ref[:, lanes_of(place, vw)] = back[b]

    for p in range(team):

        @pl.when(place != p)
        def _():
            remote(
                back.at[p], out_ref.at[:, pl.ds(p * vw, vw)], back_send.at[p], back_recv.at[p], base + p
            ).wait_recv()
            home(p, base + p).wait_send()

    for copies in sends:
        for copy in copies:
            copy.wait_send()

    @pl.when(tail_place & jnp.logical_not(last))
    def _():
        for p in range(team):
            for i in range(len(streams)):
                rim(p, base + team + p, i).wait_send()

    @pl.when(jnp.logical_not(last))
    def _():
        for h in range(hpm):
            hop(h, me + team).wait_send()


def per_device(n, q_raw, k_raw, v_raw, gate_z, beta_logit, decay_in, conv_q, conv_k, conv_v, a_log, dt_bias, norm_gain):
    size = norm_gain.shape[0]
    rows, width = q_raw.shape
    vwidth = v_raw.shape[1]
    heads = vwidth // size
    taps = conv_q.shape[0]
    team = math.gcd(n, width // size)
    kw, vw = width // team, vwidth // team
    hpm = vw // size
    units = team * hpm
    long = RIM + team * rows
    dma = pltpu.SemaphoreType.DMA
    normed = pl.pallas_call(
        functools.partial(mixer_kernel, "context", n, team, size),
        out_shape=jax.ShapeDtypeStruct((rows, vwidth), BF),
        in_specs=[pl.BlockSpec(memory_space=pltpu.HBM)] * 11,
        out_specs=pl.BlockSpec(memory_space=pltpu.VMEM),
        scratch_shapes=[
            pltpu.VMEM((long, kw), BF),
            pltpu.VMEM((long, kw), BF),
            pltpu.VMEM((long, vw), BF),
            pltpu.VMEM((team, heads, rows), F32),
            pltpu.VMEM((team, heads, rows), F32),
            pltpu.VMEM((taps, kw), BF),
            pltpu.VMEM((taps, kw), BF),
            pltpu.VMEM((taps, vw), BF),
            pltpu.VMEM((1, heads), F32),
            pltpu.VMEM((1, heads), F32),
            pltpu.VMEM((1, size), F32),
            pltpu.VMEM((long, kw), F32),
            pltpu.VMEM((long, kw), F32),
            pltpu.VMEM((long, vw), F32),
            pltpu.VMEM((units, size, size), BF),
            pltpu.VMEM((units, size), F32),
            pltpu.VMEM((units, size, size), F32),
            pltpu.VMEM((units, rows, rows), F32),
            pltpu.VMEM((units, rows, 2 * size), BF),
            pltpu.VMEM((units, size, size), BF),
            pltpu.VMEM((hpm, size, size), BF),
            pltpu.VMEM((hpm, size, size), BF),
            pltpu.VMEM((team, rows, vw), BF),
            dma((11,)),
            dma((team, 5)),
            dma((team, 5)),
            dma((team, 3)),
            dma((3,)),
            dma((hpm,)),
            dma((hpm,)),
            dma((team,)),
            dma((team,)),
        ],
        compiler_params=pltpu.CompilerParams(
            collective_id=0, has_side_effects=True, vmem_limit_bytes=60 << 20
        ),
        name="mixer",
    )(
        q_raw, k_raw, v_raw, beta_logit.T, decay_in.T, conv_q, conv_k, conv_v,
        a_log[None], dt_bias[None], norm_gain[None],
    )
    return (normed.astype(F32) * jax.nn.silu(gate_z.astype(F32))).astype(BF)


def solution(mesh):
    rows = P(("groups", "context"), "tensor")
    return jax.shard_map(
        functools.partial(per_device, mesh.shape["context"]),
        mesh=mesh,
        in_specs=(rows,) * 6 + (P(None, "tensor"),) * 3 + (P("tensor"),) * 2 + (P(),),
        out_specs=rows,
        check_vma=False,
    )
```

```python
import functools
import math

import jax
import jax.numpy as jnp
from jax import lax
from jax.experimental import pallas as pl
from jax.experimental.pallas import tpu as pltpu
from jax.sharding import PartitionSpec as P

MESH = pl.DeviceIdType.MESH
HIGH = lax.Precision.HIGHEST
RIM = 16
BF = jnp.bfloat16
F32 = jnp.float32


def mm(a, b):
    return jnp.dot(a.astype(BF), b.astype(BF), preferred_element_type=F32)


def mm_nt(a, b):
    return lax.dot_general(a.astype(BF), b.astype(BF), (((1,), (1,)), ((), ())), preferred_element_type=F32)


def mm_tn(a, b):
    return jnp.dot(a.astype(BF).T, b.astype(BF), preferred_element_type=F32)


def conv_silu(full, weights, count):
    taps = weights.shape[0]
    total = weights[0:1].astype(F32) * full(0)
    for i in range(1, taps):
        total = total + weights[i : i + 1].astype(F32) * full(i)
    return (total * jax.nn.sigmoid(total)).astype(BF)


def norm(block):
    block = block.astype(F32)
    return 1.0 / jnp.sqrt(jnp.sum(block * block, axis=-1, keepdims=True) + 1e-06)


def masks(rows):
    row = lax.broadcasted_iota(jnp.int32, (rows, rows), 0)
    col = lax.broadcasted_iota(jnp.int32, (rows, rows), 1)
    return row, col


def key_stage(ks, beta_rows, decay_rows, repeat):
    rows = ks[0].shape[0]
    units = beta_rows.shape[0]
    row, col = masks(rows)
    later = row >= col
    cum_rows = jnp.dot(decay_rows, (row <= col).astype(F32), precision=HIGH, preferred_element_type=F32)
    pad = jnp.zeros((rows - 2 * units, rows), F32)
    columns = jnp.concatenate([cum_rows, beta_rows, pad], axis=0).T
    cum, beta = columns[:, :units], columns[:, units : 2 * units]
    kn = [norm(k) for k in ks]
    kn_rows = jnp.zeros((rows, rows), F32)
    for j, column in enumerate(kn):
        kn_rows = jnp.where(col == j, column, kn_rows)
    kn_rows = kn_rows.T
    inner = [mm_nt(k, k) for k in ks]
    lower, ratios = [], []
    for h in range(units):
        j = h // repeat
        ratio = jnp.exp(jnp.minimum(cum[:, h : h + 1] - cum_rows[h : h + 1], 0.0))
        ratio = jnp.where(later, ratio, 0.0) * kn_rows[j : j + 1]
        lower.append(jnp.where(row > col, ratio * inner[j] * (beta[:, h : h + 1] * kn[j]), 0.0))
        ratios.append(ratio)
    eye = (row == col).astype(F32)
    apart = row ^ col
    inv = [eye - jnp.where(apart == 1, m, 0.0) for m in lower]
    step = 2
    while step < rows:
        mask = (apart >= step) & (apart < 2 * step)
        edge = [mm(jnp.where(mask, lower[h], 0.0), inv[h]) for h in range(units)]
        inv = [inv[h] - mm(inv[h], edge[h]) for h in range(units)]
        step *= 2
    return cum, cum_rows, kn, kn_rows, ratios, inv


def mixer_kernel(
    axis, n, team, size,
    q_ref, k_ref, v_ref, bl_ref, di_ref, wq_ref, wk_ref, wv_ref, al_ref, dt_ref, gain_ref,
    out_ref,
    q_rows, k_rows, v_rows, logits, inputs, wq, wk, wv, al, dt, gain,
    fq, fk, fv, m_s, g_s, b_s, r_s, w_s, s_s, p_s, o_s, held, sent, back,
    local_sem, send_sem, recv_sem, rim_send, rim_recv, hop_send, hop_recv, back_send, back_recv,
):
    me = lax.axis_index(axis)
    place, turn = lax.rem(me, team), me // team
    base = turn * team
    rows = q_ref.shape[0]
    taps = wq_ref.shape[0]
    kw, vw = wq_ref.shape[1] // team, wv_ref.shape[1] // team
    kpm, hpm = kw // size, vw // size
    repeat = hpm // kpm
    units = team * hpm
    first, last = turn == 0, turn == n // team - 1
    tail_place = place == team - 1
    streams = ((k_ref, k_rows, kw), (v_ref, v_rows, vw), (q_ref, q_rows, kw))
    plans = ((k_rows, wk, fk, kpm), (v_rows, wv, fv, hpm), (q_rows, wq, fq, kpm))
    whole = ((bl_ref, logits), (di_ref, inputs))

    def lanes_of(who, width):
        return pl.ds(pl.multiple_of(who * width, width), width)

    def rows_of(who):
        return pl.ds(pl.multiple_of(RIM + who * rows, RIM), rows)

    staying = []
    for i, (src, dst, width) in enumerate(streams):
        staying.append((src.at[:, lanes_of(place, width)], dst.at[rows_of(place), :]))
    for src, dst in whole:
        staying.append((src, dst.at[place]))
    for src, dst, width in ((wq_ref, wq, kw), (wk_ref, wk, kw), (wv_ref, wv, vw)):
        staying.append((src.at[:, lanes_of(place, width)], dst))
    staying += [(al_ref, al), (dt_ref, dt), (gain_ref, gain)]
    staying = [pltpu.make_async_copy(a, b, local_sem.at[i]) for i, (a, b) in enumerate(staying)]
    for copy in staying:
        copy.start()

    barrier = pltpu.get_barrier_semaphore()

    def greet(who):
        pl.semaphore_signal(barrier, inc=1, device_id={axis: who}, device_id_type=MESH)

    for d in range(1, team):
        greet(base + lax.rem(place + d, team))

    @pl.when(jnp.logical_not(last))
    def _():
        greet(me + team)

        @pl.when(tail_place)
        def _():
            for p in range(team - 1):
                greet(base + team + p)

    @pl.when(jnp.logical_not(first))
    def _():
        greet(me - team)

        @pl.when(jnp.logical_not(tail_place))
        def _():
            greet(base - 1)

    ahead = jnp.where(tail_place, team, 1)
    behind = jnp.where(tail_place, 1, 2)
    pl.semaphore_wait(barrier, team - 1 + jnp.where(last, 0, ahead) + jnp.where(first, 0, behind))

    def remote(src, dst, send, recv, to):
        return pltpu.make_async_remote_copy(
            src_ref=src, dst_ref=dst, send_sem=send, recv_sem=recv, device_id={axis: to}, device_id_type=MESH
        )

    def exchange(d):
        to = lax.rem(place + d, team)
        pairs = [(src.at[:, lanes_of(to, width)], dst.at[rows_of(place), :]) for src, dst, width in streams]
        pairs += [(src, dst.at[place]) for src, dst in whole]
        return [
            remote(a, b, send_sem.at[d - 1, i], recv_sem.at[d - 1, i], base + to) for i, (a, b) in enumerate(pairs)
        ]

    def arrival(d):
        who = lax.rem(place + team - d, team)
        pairs = [(src.at[:, lanes_of(place, width)], dst.at[rows_of(who), :]) for src, dst, width in streams]
        pairs += [(src, dst.at[who]) for src, dst in whole]
        return [
            remote(a, b, send_sem.at[d - 1, i], recv_sem.at[d - 1, i], base + who) for i, (a, b) in enumerate(pairs)
        ]

    def rim(p, to, i):
        src, dst, width = streams[i]
        return remote(
            src.at[pl.ds(rows - RIM, RIM), pl.ds(p * width, width)], dst.at[pl.ds(0, RIM), :],
            rim_send.at[p, i], rim_recv.at[i], to,
        )

    sends = [exchange(d) for d in range(1, team)]
    takes = [arrival(d) for d in range(1, team)]
    order = (3, 4, 0, 1, 2)
    for i in order:
        for copies in sends:
            copies[i].start()
        if i < len(streams):

            @pl.when(tail_place & jnp.logical_not(last))
            def _():
                for p in range(team):
                    rim(p, base + team + p, i).start()

    @pl.when(first)
    def _():
        for _, dst, _ in streams:
            dst[pl.ds(0, RIM), :] = jnp.zeros((RIM, dst.shape[1]), BF)

    for copy in staying[len(streams) :]:
        copy.wait()
    for i in (3, 4):
        for copies in takes:
            copies[i].wait_recv()

    def stream(i):
        staying[i].wait()

        @pl.when(jnp.logical_not(first))
        def _():
            rim(0, base - 1, i).wait_recv()

        for copies in takes:
            copies[i].wait_recv()
        src, w_ref, f_ref, count = plans[i]
        f_ref[...] = src[...].astype(F32)
        parts = []
        for b in range(team):
            for c in range(count):
                lanes = pl.ds(c * size, size)
                parts.append(
                    conv_silu(
                        lambda i: f_ref[pl.ds(RIM - taps + 1 + i + b * rows, rows), lanes], w_ref[:, lanes], rows
                    )
                )
        return parts

    heads = bl_ref.shape[0]
    diag = lax.broadcasted_iota(jnp.int32, (heads, heads), 0) == lax.broadcasted_iota(jnp.int32, (heads, heads), 1)

    def upright(ref):
        return jnp.sum(jnp.where(diag, ref[...], 0.0), axis=1, keepdims=True)

    scale_up, shift = jnp.exp(upright(al)), upright(dt)
    beta_rows, decay_rows = [], []
    for b in range(team):
        x = inputs[b] + shift
        decay = -scale_up * (jnp.maximum(x, 0.0) + jnp.log1p(jnp.exp(-jnp.abs(x))))
        beta = jax.nn.sigmoid(logits[b])
        for h in range(hpm):
            pick_b, pick_d = beta[h : h + 1], decay[h : h + 1]
            for p in range(1, team):
                at = p * hpm + h
                pick_b = jnp.where(place == p, beta[at : at + 1], pick_b)
                pick_d = jnp.where(place == p, decay[at : at + 1], pick_d)
            beta_rows.append(pick_b)
            decay_rows.append(pick_d)
    beta_rows = jnp.concatenate(beta_rows, axis=0)
    decay_rows = jnp.concatenate(decay_rows, axis=0)
    ks = stream(0)
    cum, cum_rows, kn, kn_rows, ratios, inv = key_stage(ks, beta_rows, decay_rows, repeat)
    growth = jnp.exp(cum)
    tail = jnp.exp(cum[rows - 1 : rows] - cum)
    for u in range(units):
        r_s[u] = ratios[u]
        beta_row = beta_rows[u : u + 1]
        gain_row = beta_row * jnp.exp(cum_rows[u : u + 1]) * kn_rows[u // repeat : u // repeat + 1]
        w_s[u, :, pl.ds(0, size)] = mm(inv[u] * gain_row, ks[u // repeat]).astype(BF)
    inv = [(inv[u] * beta_rows[u : u + 1]).astype(BF) for u in range(units)]
    vs = stream(1)
    for u in range(units):
        w_s[u, :, pl.ds(size, size)] = mm(inv[u], vs[u]).astype(BF)
    for u in range(units):
        key_tail = (ks[u // repeat].astype(F32) * (kn[u // repeat] * tail[:, u : u + 1])).astype(BF)
        ends = mm_tn(key_tail, w_s[u])
        m_s[u] = (-ends[:, :size]).astype(BF)
        b_s[u] = ends[:, size:]
        g_s[pl.ds(u, 1), :] = jnp.broadcast_to(growth[rows - 1 : rows, u : u + 1], (1, size))

    def hop(h, to):
        return remote(sent.at[h], held.at[h], hop_send.at[h], hop_recv.at[h], to)

    def onward(states):
        @pl.when(jnp.logical_not(last))
        def _():
            for h in range(hpm):
                sent[h] = states[h].astype(BF)
                hop(h, me + team).start()

    @pl.when(first)
    def _():
        states = [b_s[h] for h in range(hpm)]
        for h in range(hpm):
            s_s[h] = jnp.zeros((size, size), BF)
        for b in range(1, team):
            for h in range(hpm):
                u = b * hpm + h
                low = states[h].astype(BF)
                s_s[u] = low
                states[h] = (
                    b_s[u] + g_s[pl.ds(u, 1), :] * states[h] + jnp.dot(m_s[u], low, preferred_element_type=F32)
                )
        onward(states)

    qs = stream(2)
    cross = [mm_nt(q, k) for q, k in zip(qs, ks)]
    qn = [norm(q) * size ** (-0.5) for q in qs]
    for u in range(units):
        j = u // repeat
        inside = mm(r_s[u] * cross[j] * qn[j], w_s[u])
        p_s[u] = (qs[j].astype(F32) * (qn[j] * growth[:, u : u + 1]) - inside[:, :size]).astype(BF)
        o_s[u] = inside[:, size:]

    @pl.when(jnp.logical_not(first))
    def _():
        row, col = masks(size)
        eye = (row == col).astype(F32)
        turns = [g_s[pl.ds(h, 1), :] * eye + m_s[h].astype(F32) for h in range(hpm)]
        adds = [b_s[h] for h in range(hpm)]
        for b in range(1, team):
            for h in range(hpm):
                u = b * hpm + h
                low = jnp.concatenate([turns[h].astype(BF), adds[h].astype(BF)], axis=1)
                end = g_s[pl.ds(u, 1), :]
                moved = jnp.dot(m_s[u], low, preferred_element_type=F32)
                seen = jnp.dot(p_s[u], low, preferred_element_type=F32)
                p_s[u] = seen[:, :size].astype(BF)
                o_s[u] = o_s[u] + seen[:, size:]
                turns[h] = end * turns[h] + moved[:, :size]
                adds[h] = b_s[u] + end * adds[h] + moved[:, size:]
        for h in range(hpm):
            m_s[h] = turns[h].astype(BF)
            b_s[h] = adds[h]
        for h in range(hpm):
            hop(h, me - team).wait_recv()

        @pl.when(jnp.logical_not(last))
        def _():
            onward([b_s[h] + jnp.dot(m_s[h], held[h], preferred_element_type=F32) for h in range(hpm)])

        for u in range(units):
            s_s[u] = held[u % hpm]

    def home(b, to):
        return remote(back.at[b], out_ref.at[:, lanes_of(place, vw)], back_send.at[b], back_recv.at[place], to)

    for b in range(team):
        for h in range(hpm):
            u = b * hpm + h
            mixed = o_s[u] + jnp.dot(p_s[u], s_s[u], preferred_element_type=F32)
            scale = lax.rsqrt(jnp.mean(mixed * mixed, axis=-1, keepdims=True) + 1e-06)
            back[b, :, pl.ds(h * size, size)] = (mixed * scale * gain[...]).astype(BF)

        @pl.when(place != b)
        def _():
            home(b, base + b).start()

        @pl.when(place == b)
        def _():
            out_ref[:, lanes_of(place, vw)] = back[b]

    for p in range(team):

        @pl.when(place != p)
        def _():
            remote(
                back.at[p], out_ref.at[:, pl.ds(p * vw, vw)], back_send.at[p], back_recv.at[p], base + p
            ).wait_recv()
            home(p, base + p).wait_send()

    for copies in sends:
        for copy in copies:
            copy.wait_send()

    @pl.when(tail_place & jnp.logical_not(last))
    def _():
        for p in range(team):
            for i in range(len(streams)):
                rim(p, base + team + p, i).wait_send()

    @pl.when(jnp.logical_not(last))
    def _():
        for h in range(hpm):
            hop(h, me + team).wait_send()


def per_device(n, q_raw, k_raw, v_raw, gate_z, beta_logit, decay_in, conv_q, conv_k, conv_v, a_log, dt_bias, norm_gain):
    size = norm_gain.shape[0]
    rows, width = q_raw.shape
    vwidth = v_raw.shape[1]
    heads = vwidth // size
    taps = conv_q.shape[0]
    team = math.gcd(n, width // size)
    kw, vw = width // team, vwidth // team
    hpm = vw // size
    units = team * hpm
    long = RIM + team * rows
    dma = pltpu.SemaphoreType.DMA
    normed = pl.pallas_call(
        functools.partial(mixer_kernel, "context", n, team, size),
        out_shape=jax.ShapeDtypeStruct((rows, vwidth), BF),
        in_specs=[pl.BlockSpec(memory_space=pltpu.HBM)] * 11,
        out_specs=pl.BlockSpec(memory_space=pltpu.VMEM),
        scratch_shapes=[
            pltpu.VMEM((long, kw), BF),
            pltpu.VMEM((long, kw), BF),
            pltpu.VMEM((long, vw), BF),
            pltpu.VMEM((team, heads, rows), F32),
            pltpu.VMEM((team, heads, rows), F32),
            pltpu.VMEM((taps, kw), BF),
            pltpu.VMEM((taps, kw), BF),
            pltpu.VMEM((taps, vw), BF),
            pltpu.VMEM((1, heads), F32),
            pltpu.VMEM((1, heads), F32),
            pltpu.VMEM((1, size), F32),
            pltpu.VMEM((long, kw), F32),
            pltpu.VMEM((long, kw), F32),
            pltpu.VMEM((long, vw), F32),
            pltpu.VMEM((units, size, size), BF),
            pltpu.VMEM((units, size), F32),
            pltpu.VMEM((units, size, size), F32),
            pltpu.VMEM((units, rows, rows), F32),
            pltpu.VMEM((units, rows, 2 * size), BF),
            pltpu.VMEM((units, size, size), BF),
            pltpu.VMEM((units, rows, size), BF),
            pltpu.VMEM((units, rows, size), F32),
            pltpu.VMEM((hpm, size, size), BF),
            pltpu.VMEM((hpm, size, size), BF),
            pltpu.VMEM((team, rows, vw), BF),
            dma((11,)),
            dma((team, 5)),
            dma((team, 5)),
            dma((team, 3)),
            dma((3,)),
            dma((hpm,)),
            dma((hpm,)),
            dma((team,)),
            dma((team,)),
        ],
        compiler_params=pltpu.CompilerParams(
            collective_id=0, has_side_effects=True, vmem_limit_bytes=60 << 20
        ),
        name="mixer",
    )(
        q_raw, k_raw, v_raw, beta_logit.T, decay_in.T, conv_q, conv_k, conv_v,
        a_log[None], dt_bias[None], norm_gain[None],
    )
    return (normed.astype(F32) * jax.nn.silu(gate_z.astype(F32))).astype(BF)


def solution(mesh):
    rows = P(("groups", "context"), "tensor")
    return jax.shard_map(
        functools.partial(per_device, mesh.shape["context"]),
        mesh=mesh,
        in_specs=(rows,) * 6 + (P(None, "tensor"),) * 3 + (P("tensor"),) * 2 + (P(),),
        out_specs=rows,
        check_vma=False,
    )
```

```python
import functools
import math

import jax
import jax.numpy as jnp
from jax import lax
from jax.experimental import pallas as pl
from jax.experimental.pallas import tpu as pltpu
from jax.sharding import PartitionSpec as P

MESH = pl.DeviceIdType.MESH
HIGH = lax.Precision.HIGHEST
RIM = 16
BF = jnp.bfloat16
F32 = jnp.float32


def mm(a, b):
    return jnp.dot(a.astype(BF), b.astype(BF), preferred_element_type=F32)


def mm_nt(a, b):
    return lax.dot_general(a.astype(BF), b.astype(BF), (((1,), (1,)), ((), ())), preferred_element_type=F32)


def mm_tn(a, b):
    return jnp.dot(a.astype(BF).T, b.astype(BF), preferred_element_type=F32)


def conv_silu(full, weights, count):
    taps = weights.shape[0]
    total = weights[0:1].astype(F32) * full(0)
    for i in range(1, taps):
        total = total + weights[i : i + 1].astype(F32) * full(i)
    return (total * jax.nn.sigmoid(total)).astype(BF)


def norm(block):
    block = block.astype(F32)
    return 1.0 / jnp.sqrt(jnp.sum(block * block, axis=-1, keepdims=True) + 1e-06)


def masks(rows):
    row = lax.broadcasted_iota(jnp.int32, (rows, rows), 0)
    col = lax.broadcasted_iota(jnp.int32, (rows, rows), 1)
    return row, col


def decay_stage(beta_rows, decay_rows):
    units, rows = beta_rows.shape
    row, col = masks(rows)
    cum_rows = jnp.dot(decay_rows, (row <= col).astype(F32), precision=HIGH, preferred_element_type=F32)
    pad = jnp.zeros((rows - 2 * units, rows), F32)
    columns = jnp.concatenate([cum_rows, beta_rows, pad], axis=0).T
    return cum_rows, columns[:, :units], columns[:, units : 2 * units]


def key_stage(ks, beta, decays, repeat):
    rows = ks[0].shape[0]
    units = beta.shape[1]
    row, col = masks(rows)
    kn = [norm(k) for k in ks]
    kn_rows = jnp.zeros((rows, rows), F32)
    for j, column in enumerate(kn):
        kn_rows = jnp.where(col == j, column, kn_rows)
    kn_rows = kn_rows.T
    inner = [mm_nt(k, k) for k in ks]
    lower, ratios = [], []
    for h in range(units):
        j = h // repeat
        ratio = decays[h] * kn_rows[j : j + 1]
        lower.append(jnp.where(row > col, ratio * inner[j] * (beta[:, h : h + 1] * kn[j]), 0.0))
        ratios.append(ratio)
    eye = (row == col).astype(F32)
    apart = row ^ col
    inv = [eye - jnp.where(apart == 1, m, 0.0) for m in lower]
    step = 2
    while step < rows:
        mask = (apart >= step) & (apart < 2 * step)
        edge = [mm(jnp.where(mask, lower[h], 0.0), inv[h]) for h in range(units)]
        inv = [inv[h] - mm(inv[h], edge[h]) for h in range(units)]
        step *= 2
    return kn, kn_rows, ratios, inv


def mixer_kernel(
    axis, n, team, size,
    q_ref, k_ref, v_ref, bl_ref, di_ref, wq_ref, wk_ref, wv_ref, al_ref, dt_ref, gain_ref,
    out_ref,
    q_rows, k_rows, v_rows, logits, inputs, wq, wk, wv, al, dt, gain,
    fq, fk, fv, m_s, g_s, b_s, r_s, w_s, s_s, p_s, o_s, held, sent, back,
    local_sem, send_sem, recv_sem, rim_send, rim_recv, hop_send, hop_recv, back_send, back_recv,
):
    me = lax.axis_index(axis)
    place, turn = lax.rem(me, team), me // team
    base = turn * team
    rows = q_ref.shape[0]
    taps = wq_ref.shape[0]
    kw, vw = wq_ref.shape[1] // team, wv_ref.shape[1] // team
    kpm, hpm = kw // size, vw // size
    repeat = hpm // kpm
    units = team * hpm
    first, last = turn == 0, turn == n // team - 1
    tail_place = place == team - 1
    streams = ((k_ref, k_rows, kw), (v_ref, v_rows, vw), (q_ref, q_rows, kw))
    plans = ((k_rows, wk, fk, kpm), (v_rows, wv, fv, hpm), (q_rows, wq, fq, kpm))
    whole = ((bl_ref, logits), (di_ref, inputs))

    def lanes_of(who, width):
        return pl.ds(pl.multiple_of(who * width, width), width)

    def rows_of(who):
        return pl.ds(pl.multiple_of(RIM + who * rows, RIM), rows)

    staying = []
    for i, (src, dst, width) in enumerate(streams):
        staying.append((src.at[:, lanes_of(place, width)], dst.at[rows_of(place), :]))
    for src, dst in whole:
        staying.append((src, dst.at[place]))
    for src, dst, width in ((wq_ref, wq, kw), (wk_ref, wk, kw), (wv_ref, wv, vw)):
        staying.append((src.at[:, lanes_of(place, width)], dst))
    staying += [(al_ref, al), (dt_ref, dt), (gain_ref, gain)]
    staying = [pltpu.make_async_copy(a, b, local_sem.at[i]) for i, (a, b) in enumerate(staying)]
    for copy in staying:
        copy.start()

    barrier = pltpu.get_barrier_semaphore()

    def greet(who):
        pl.semaphore_signal(barrier, inc=1, device_id={axis: who}, device_id_type=MESH)

    for d in range(1, team):
        greet(base + lax.rem(place + d, team))

    @pl.when(jnp.logical_not(last))
    def _():
        greet(me + team)

        @pl.when(tail_place)
        def _():
            for p in range(team - 1):
                greet(base + team + p)

    @pl.when(jnp.logical_not(first))
    def _():
        greet(me - team)

        @pl.when(jnp.logical_not(tail_place))
        def _():
            greet(base - 1)

    ahead = jnp.where(tail_place, team, 1)
    behind = jnp.where(tail_place, 1, 2)
    pl.semaphore_wait(barrier, team - 1 + jnp.where(last, 0, ahead) + jnp.where(first, 0, behind))

    def remote(src, dst, send, recv, to):
        return pltpu.make_async_remote_copy(
            src_ref=src, dst_ref=dst, send_sem=send, recv_sem=recv, device_id={axis: to}, device_id_type=MESH
        )

    def exchange(d):
        to = lax.rem(place + d, team)
        pairs = [(src.at[:, lanes_of(to, width)], dst.at[rows_of(place), :]) for src, dst, width in streams]
        pairs += [(src, dst.at[place]) for src, dst in whole]
        return [
            remote(a, b, send_sem.at[d - 1, i], recv_sem.at[d - 1, i], base + to) for i, (a, b) in enumerate(pairs)
        ]

    def arrival(d):
        who = lax.rem(place + team - d, team)
        pairs = [(src.at[:, lanes_of(place, width)], dst.at[rows_of(who), :]) for src, dst, width in streams]
        pairs += [(src, dst.at[who]) for src, dst in whole]
        return [
            remote(a, b, send_sem.at[d - 1, i], recv_sem.at[d - 1, i], base + who) for i, (a, b) in enumerate(pairs)
        ]

    def rim(p, to, i):
        src, dst, width = streams[i]
        return remote(
            src.at[pl.ds(rows - RIM, RIM), pl.ds(p * width, width)], dst.at[pl.ds(0, RIM), :],
            rim_send.at[p, i], rim_recv.at[i], to,
        )

    sends = [exchange(d) for d in range(1, team)]
    takes = [arrival(d) for d in range(1, team)]
    order = (3, 4, 0, 1, 2)
    for i in order:
        for copies in sends:
            copies[i].start()
        if i < len(streams):

            @pl.when(tail_place & jnp.logical_not(last))
            def _():
                for p in range(team):
                    rim(p, base + team + p, i).start()

    @pl.when(first)
    def _():
        for _, dst, _ in streams:
            dst[pl.ds(0, RIM), :] = jnp.zeros((RIM, dst.shape[1]), BF)

    for copy in staying[len(streams) :]:
        copy.wait()
    for i in (3, 4):
        for copies in takes:
            copies[i].wait_recv()

    def stream(i):
        staying[i].wait()

        @pl.when(jnp.logical_not(first))
        def _():
            rim(0, base - 1, i).wait_recv()

        for copies in takes:
            copies[i].wait_recv()
        src, w_ref, f_ref, count = plans[i]
        f_ref[...] = src[...].astype(F32)
        parts = []
        for b in range(team):
            for c in range(count):
                lanes = pl.ds(c * size, size)
                parts.append(
                    conv_silu(
                        lambda i: f_ref[pl.ds(RIM - taps + 1 + i + b * rows, rows), lanes], w_ref[:, lanes], rows
                    )
                )
        return parts

    heads = bl_ref.shape[0]
    diag = lax.broadcasted_iota(jnp.int32, (heads, heads), 0) == lax.broadcasted_iota(jnp.int32, (heads, heads), 1)

    def upright(ref):
        return jnp.sum(jnp.where(diag, ref[...], 0.0), axis=1, keepdims=True)

    scale_up, shift = jnp.exp(upright(al)), upright(dt)
    beta_rows, decay_rows = [], []
    for b in range(team):
        x = inputs[b] + shift
        decay = -scale_up * (jnp.maximum(x, 0.0) + jnp.log1p(jnp.exp(-jnp.abs(x))))
        beta = jax.nn.sigmoid(logits[b])
        for h in range(hpm):
            pick_b, pick_d = beta[h : h + 1], decay[h : h + 1]
            for p in range(1, team):
                at = p * hpm + h
                pick_b = jnp.where(place == p, beta[at : at + 1], pick_b)
                pick_d = jnp.where(place == p, decay[at : at + 1], pick_d)
            beta_rows.append(pick_b)
            decay_rows.append(pick_d)
    beta_rows = jnp.concatenate(beta_rows, axis=0)
    decay_rows = jnp.concatenate(decay_rows, axis=0)
    cum_rows, cum, beta = decay_stage(beta_rows, decay_rows)
    growth = jnp.exp(cum)
    tail = jnp.exp(cum[rows - 1 : rows] - cum)
    row, col = masks(rows)
    for u in range(units):
        ratio = jnp.exp(jnp.minimum(cum[:, u : u + 1] - cum_rows[u : u + 1], 0.0))
        r_s[u] = jnp.where(row >= col, ratio, 0.0)
    ks = stream(0)
    kn, kn_rows, ratios, inv = key_stage(ks, beta, [r_s[u] for u in range(units)], repeat)
    for u in range(units):
        r_s[u] = ratios[u]
        beta_row = beta_rows[u : u + 1]
        gain_row = beta_row * jnp.exp(cum_rows[u : u + 1]) * kn_rows[u // repeat : u // repeat + 1]
        w_s[u, :, pl.ds(0, size)] = mm(inv[u] * gain_row, ks[u // repeat]).astype(BF)
    inv = [(inv[u] * beta_rows[u : u + 1]).astype(BF) for u in range(units)]
    vs = stream(1)
    for u in range(units):
        w_s[u, :, pl.ds(size, size)] = mm(inv[u], vs[u]).astype(BF)
    for u in range(units):
        key_tail = (ks[u // repeat].astype(F32) * (kn[u // repeat] * tail[:, u : u + 1])).astype(BF)
        ends = mm_tn(key_tail, w_s[u])
        m_s[u] = (-ends[:, :size]).astype(BF)
        b_s[u] = ends[:, size:]
        g_s[pl.ds(u, 1), :] = jnp.broadcast_to(growth[rows - 1 : rows, u : u + 1], (1, size))

    def hop(h, to):
        return remote(sent.at[h], held.at[h], hop_send.at[h], hop_recv.at[h], to)

    def onward(states):
        @pl.when(jnp.logical_not(last))
        def _():
            for h in range(hpm):
                sent[h] = states[h].astype(BF)
                hop(h, me + team).start()

    @pl.when(first)
    def _():
        states = [b_s[h] for h in range(hpm)]
        for h in range(hpm):
            s_s[h] = jnp.zeros((size, size), BF)
        for b in range(1, team):
            for h in range(hpm):
                u = b * hpm + h
                low = states[h].astype(BF)
                s_s[u] = low
                states[h] = (
                    b_s[u] + g_s[pl.ds(u, 1), :] * states[h] + jnp.dot(m_s[u], low, preferred_element_type=F32)
                )
        onward(states)

    qs = stream(2)
    cross = [mm_nt(q, k) for q, k in zip(qs, ks)]
    qn = [norm(q) * size ** (-0.5) for q in qs]
    for u in range(units):
        j = u // repeat
        inside = mm(r_s[u] * cross[j] * qn[j], w_s[u])
        p_s[u] = (qs[j].astype(F32) * (qn[j] * growth[:, u : u + 1]) - inside[:, :size]).astype(BF)
        o_s[u] = inside[:, size:]

    @pl.when(jnp.logical_not(first))
    def _():
        row, col = masks(size)
        eye = (row == col).astype(F32)
        turns = [g_s[pl.ds(h, 1), :] * eye + m_s[h].astype(F32) for h in range(hpm)]
        adds = [b_s[h] for h in range(hpm)]
        for b in range(1, team):
            for h in range(hpm):
                u = b * hpm + h
                low = jnp.concatenate([turns[h].astype(BF), adds[h].astype(BF)], axis=1)
                end = g_s[pl.ds(u, 1), :]
                moved = jnp.dot(m_s[u], low, preferred_element_type=F32)
                seen = jnp.dot(p_s[u], low, preferred_element_type=F32)
                p_s[u] = seen[:, :size].astype(BF)
                o_s[u] = o_s[u] + seen[:, size:]
                turns[h] = end * turns[h] + moved[:, :size]
                adds[h] = b_s[u] + end * adds[h] + moved[:, size:]
        for h in range(hpm):
            m_s[h] = turns[h].astype(BF)
            b_s[h] = adds[h]
        for h in range(hpm):
            hop(h, me - team).wait_recv()

        @pl.when(jnp.logical_not(last))
        def _():
            onward([b_s[h] + jnp.dot(m_s[h], held[h], preferred_element_type=F32) for h in range(hpm)])

        for u in range(units):
            s_s[u] = held[u % hpm]

    def home(b, to):
        return remote(back.at[b], out_ref.at[:, lanes_of(place, vw)], back_send.at[b], back_recv.at[place], to)

    for b in range(team):
        for h in range(hpm):
            u = b * hpm + h
            mixed = o_s[u] + jnp.dot(p_s[u], s_s[u], preferred_element_type=F32)
            scale = lax.rsqrt(jnp.mean(mixed * mixed, axis=-1, keepdims=True) + 1e-06)
            back[b, :, pl.ds(h * size, size)] = (mixed * scale * gain[...]).astype(BF)

        @pl.when(place != b)
        def _():
            home(b, base + b).start()

        @pl.when(place == b)
        def _():
            pltpu.make_async_copy(back.at[b], out_ref.at[:, lanes_of(place, vw)], back_recv.at[place]).start()

    for p in range(team):

        @pl.when(place != p)
        def _():
            remote(
                back.at[p], out_ref.at[:, pl.ds(p * vw, vw)], back_send.at[p], back_recv.at[p], base + p
            ).wait_recv()
            home(p, base + p).wait_send()

        @pl.when(place == p)
        def _():
            pltpu.make_async_copy(back.at[p], out_ref.at[:, lanes_of(place, vw)], back_recv.at[place]).wait()

    for copies in sends:
        for copy in copies:
            copy.wait_send()

    @pl.when(tail_place & jnp.logical_not(last))
    def _():
        for p in range(team):
            for i in range(len(streams)):
                rim(p, base + team + p, i).wait_send()

    @pl.when(jnp.logical_not(last))
    def _():
        for h in range(hpm):
            hop(h, me + team).wait_send()


def per_device(n, q_raw, k_raw, v_raw, gate_z, beta_logit, decay_in, conv_q, conv_k, conv_v, a_log, dt_bias, norm_gain):
    size = norm_gain.shape[0]
    rows, width = q_raw.shape
    vwidth = v_raw.shape[1]
    heads = vwidth // size
    taps = conv_q.shape[0]
    team = math.gcd(n, width // size)
    kw, vw = width // team, vwidth // team
    hpm = vw // size
    units = team * hpm
    long = RIM + team * rows
    dma = pltpu.SemaphoreType.DMA
    normed = pl.pallas_call(
        functools.partial(mixer_kernel, "context", n, team, size),
        out_shape=jax.ShapeDtypeStruct((rows, vwidth), BF),
        in_specs=[pl.BlockSpec(memory_space=pltpu.HBM)] * 11,
        out_specs=pl.BlockSpec(memory_space=pltpu.HBM),
        scratch_shapes=[
            pltpu.VMEM((long, kw), BF),
            pltpu.VMEM((long, kw), BF),
            pltpu.VMEM((long, vw), BF),
            pltpu.VMEM((team, heads, rows), F32),
            pltpu.VMEM((team, heads, rows), F32),
            pltpu.VMEM((taps, kw), BF),
            pltpu.VMEM((taps, kw), BF),
            pltpu.VMEM((taps, vw), BF),
            pltpu.VMEM((1, heads), F32),
            pltpu.VMEM((1, heads), F32),
            pltpu.VMEM((1, size), F32),
            pltpu.VMEM((long, kw), F32),
            pltpu.VMEM((long, kw), F32),
            pltpu.VMEM((long, vw), F32),
            pltpu.VMEM((units, size, size), BF),
            pltpu.VMEM((units, size), F32),
            pltpu.VMEM((units, size, size), F32),
            pltpu.VMEM((units, rows, rows), F32),
            pltpu.VMEM((units, rows, 2 * size), BF),
            pltpu.VMEM((units, size, size), BF),
            pltpu.VMEM((units, rows, size), BF),
            pltpu.VMEM((units, rows, size), F32),
            pltpu.VMEM((hpm, size, size), BF),
            pltpu.VMEM((hpm, size, size), BF),
            pltpu.VMEM((team, rows, vw), BF),
            dma((11,)),
            dma((team, 5)),
            dma((team, 5)),
            dma((team, 3)),
            dma((3,)),
            dma((hpm,)),
            dma((hpm,)),
            dma((team,)),
            dma((team,)),
        ],
        compiler_params=pltpu.CompilerParams(
            collective_id=0, has_side_effects=True, vmem_limit_bytes=60 << 20
        ),
        name="mixer",
    )(
        q_raw, k_raw, v_raw, beta_logit.T, decay_in.T, conv_q, conv_k, conv_v,
        a_log[None], dt_bias[None], norm_gain[None],
    )
    return (normed.astype(F32) * jax.nn.silu(gate_z.astype(F32))).astype(BF)


def solution(mesh):
    rows = P(("groups", "context"), "tensor")
    return jax.shard_map(
        functools.partial(per_device, mesh.shape["context"]),
        mesh=mesh,
        in_specs=(rows,) * 6 + (P(None, "tensor"),) * 3 + (P("tensor"),) * 2 + (P(),),
        out_specs=rows,
        check_vma=False,
    )
```
